32 devices in a mesh: dp: 4 (over z), head: 8 (over y, x, core).
Axes of the slice: x: 2, y: 2, z: 4, core: 2. Of those that a mesh axis runs over, the one named last changes fastest.
Arguments:
- tokens: bfloat16 [6144, 1152], P('dp'), may hold values from -6 to 6
- seg_ids: int32 [4, 1536], P('dp'), may hold values from 0 to 2, as said below
- time_steps: int32 [12], P('dp'), may hold values from 0 to 999
- head_masks: int32 [12, 16], P('dp', 'head'), may hold values 0 or 1
- skip_masks: int32 [4, 1536], P('dp'), may hold values 0 or 1
- ada_weight: bfloat16 [1152, 6912], P(None, 'head'), may hold values from -0.1875 to 0.1875
- ada_bias: bfloat16 [6912], P('head'), may hold values from -3 to 3
- qkv_weight: bfloat16 [1152, 3, 1152], P(None, None, 'head'), may hold values from -0.1875 to 0.1875
- qv_bias: bfloat16 [2, 1152], P(None, 'head'), may hold values from -2 to 2
- proj_weight: bfloat16 [1152, 1152], P('head'), may hold values from -3 to 3
- proj_bias: bfloat16 [1152], replicated, may hold values from -2 to 2
- fc1_weight: bfloat16 [1152, 4608], P(None, 'head'), may hold values from -0.1875 to 0.1875
- fc1_bias: bfloat16 [4608], P('head'), may hold values from -2 to 2
- fc2_weight: bfloat16 [4608, 1152], P('head'), may hold values from -0.09375 to 0.09375
- fc2_bias: bfloat16 [1152], replicated, may hold values from -2 to 2
- out_cotangent: bfloat16 [6144, 1152], P('dp'), may hold values from -6 to 6
Outputs:
- layer_out: bfloat16 [6144, 1152], P(('dp', 'head'))
- input_grad: float32 [6144, 1152], P(('dp', 'head'))
- ada_weight_grad: float32 [1152, 6912], P(None, 'head')
- ada_bias_grad: float32 [6912], P('head')
- qkv_weight_grad: float32 [1152, 3, 1152], P(None, None, 'head')
- qv_bias_grad: float32 [2, 1152], P(None, 'head')
- proj_weight_grad: float32 [1152, 1152], P('head')
- proj_bias_grad: float32 [1152], replicated
- fc1_weight_grad: float32 [1152, 4608], P(None, 'head')
- fc1_bias_grad: float32 [4608], P('head')
- fc2_weight_grad: float32 [4608, 1152], P('head')
- fc2_bias_grad: float32 [1152], replicated
The draws below stay inside these ranges and needn't reach their ends.
Inputs may be any that keep to these rules, and one draw needn't show every extreme that they name: `seg_ids`: each pack holds one image of 1024 tokens and two images of 256 tokens, each on neighbouring positions, in an order that the draw chooses for each pack; the image numbers 0, 1, 2 never fall along a pack.
All inputs are finite; a program needn't handle non-finite values. No bound on the sum of `head_masks` or of `skip_masks` on one device may be relied on, other than what follows from the above.
Results may differ from the reference program's by a relative error of at most 0.01255.
The reference program's roundings to bfloat16 on the way count: a program that leaves them out, or rounds other values in their place, can miss the bound.
Values may be sent and summed in bfloat16 or wider, within the bound.
A program may use at most 192 MiB of HBM per device.

```python
import math
from functools import partial
import jax
import jax.numpy as jnp
from jax import lax

D = 1152
HEADS = 16
HEAD_DIM = 72
FF = 4608
LONG_LEN = 1024
SEG_DEV = 3
SHORT_LEN = 256
TOK_DEV = 1536
TOKENS = 6144
ITEMS = 12
N_DP = 4


def draw_seg_ids(key, part):
    long_place = jax.random.randint(jax.random.fold_in(key, 17), (N_DP,), 0, 3, dtype=jnp.int32)
    images = jnp.arange(3, dtype=jnp.int32)
    image_lens = jnp.where(images[None, :] == long_place[:, None], LONG_LEN, SHORT_LEN).astype(jnp.int32)
    first_end = image_lens[:, 0]
    second_end = image_lens[:, 0] + image_lens[:, 1]
    position = jnp.arange(TOK_DEV, dtype=jnp.int32)[None, :]
    seg = (position >= first_end[:, None]).astype(jnp.int32) + (position >= second_end[:, None]).astype(jnp.int32)
    return seg.astype(jnp.int32)


def set_ends(values, own_key, least, high):
    longest = values.shape.index(max(values.shape))
    spots = []
    for shift in (0, 1):
        where = [jax.random.randint(jax.random.fold_in(own_key, axis), (), 0, length) for axis, length in enumerate(values.shape)]
        where[longest] = (where[longest] + shift) % values.shape[longest]
        spots.append(tuple(where))
    return values.at[spots[0]].set(least).at[spots[1]].set(high)


def block_levels(rng, shape, shards, least, top_value):
    factor_of = 1.0
    for axis_at, shards_of in shards:
        steps = jax.random.uniform(jax.random.fold_in(jax.random.fold_in(rng, 6), axis_at), (shards_of,), jnp.float32, least / len(shards), top_value / len(shards))
        factor_of = factor_of * jnp.repeat(jnp.exp(steps), shape[axis_at] // shards_of).reshape((-1,) + (1,) * (len(shape) - 1 - axis_at))
    return factor_of


def bell_draw(own_key, shape, deviation, limit, cuts=(), held_as=jnp.bfloat16):
    drawn = deviation * jax.random.normal(own_key, shape, jnp.float32)
    if cuts:
        drawn = drawn * block_levels(own_key, shape, cuts, -0.22, 0.18)
    return jnp.clip(drawn, -limit, limit).astype(held_as)


def setup_inputs(seed: int = 0) -> dict:
    key_of = jax.random.split(jax.random.key(seed), 17)
    return {
        "tokens": bell_draw(key_of[0], (TOKENS, D), 1.0, 6.0, ((0, 4),)),
        "seg_ids": draw_seg_ids(jax.random.fold_in(key_of[16], 71), 0),
        "time_steps": set_ends(jax.random.randint(key_of[2], (ITEMS,), 0, 1000), jax.random.fold_in(key_of[2], 1), 0, 999).astype(jnp.int32),
        "head_masks": set_ends((jax.random.randint(key_of[3], (ITEMS, HEADS), 0, 4) < 3).astype(jnp.int32), jax.random.fold_in(key_of[3], 1), 0, 1),
        "skip_masks": set_ends((jax.random.randint(key_of[4], (N_DP, TOK_DEV), 0, 4) < 3).astype(jnp.int32), jax.random.fold_in(key_of[4], 1), 0, 1),
        "ada_weight": bell_draw(key_of[5], (D, 6 * D), D ** -0.5, 0.1875, ((1, 8),)),
        "ada_bias": bell_draw(key_of[6], (6 * D,), 0.5, 3.0, ((0, 8),)),
        "qkv_weight": bell_draw(key_of[7], (D, 3, HEADS * HEAD_DIM), D ** -0.5, 0.1875, ((2, 8),)),
        "qv_bias": bell_draw(key_of[8], (2, HEADS * HEAD_DIM), 0.3, 2.0, ((1, 8),)),
        "proj_weight": bell_draw(key_of[9], (HEADS * HEAD_DIM, D), (max(1, HEADS * HEAD_DIM // 256)) ** -0.5, 3.0, ((0, 8),)),
        "proj_bias": bell_draw(key_of[10], (D,), 0.3, 2.0),
        "fc1_weight": bell_draw(key_of[11], (D, FF), D ** -0.5, 0.1875, ((1, 8),)),
        "fc1_bias": bell_draw(key_of[12], (FF,), 0.3, 2.0, ((0, 8),)),
        "fc2_weight": bell_draw(key_of[13], (FF, D), FF ** -0.5, 0.09375, ((0, 8),)),
        "fc2_bias": bell_draw(key_of[14], (D,), 0.3, 2.0),
        "out_cotangent": bell_draw(key_of[15], (TOKENS, D), 1.0, 6.0, ((0, 4),)),
    }


highest = lax.Precision.HIGHEST

@jax.custom_vjp
def low(v):
    return lax.optimization_barrier(v.astype(jnp.bfloat16)).astype(jnp.float32)

@jax.custom_vjp
def low_back(v):
    return v

def low_keep(v):
    return (low(v), None)

def low_pass(kept, grad):
    return (grad,)

def back_keep(v):
    return (v, None)

def back_low(kept, grad):
    return (low(grad),)
low.defvjp(low_keep, low_pass)
low_back.defvjp(back_keep, back_low)

def embed_steps(steps):
    half_width = D // 2
    freqs = jnp.exp(-math.log(10000.0) * jnp.arange(half_width, dtype=jnp.float32) / half_width)
    angles = steps.astype(jnp.float32)[:, None] * freqs[None, :]
    return jnp.concatenate([jnp.cos(angles), jnp.sin(angles)], axis=1)

def normalize(value):
    center = value - lax.optimization_barrier(jnp.mean(value, axis=-1, keepdims=True))
    return center * lax.rsqrt(lax.optimization_barrier(jnp.mean(center * center, axis=-1, keepdims=True)) + 1e-06)

def pack_layer(weights, x_pack, seg_pack, hmask_pack, keep_pack, mod_pack):
    wqkv, bqv, wproj, bproj, wone, bone, wtwo, btwo = weights
    select = (seg_pack[:, None] == jnp.arange(SEG_DEV, dtype=jnp.int32)[None, :]).astype(jnp.float32)
    tok_mod = jnp.dot(select, mod_pack, precision=highest)
    shift_one, scale_one, gate_one, shift_two, scale_two, gate_two = jnp.split(tok_mod, 6, axis=1)
    h_one = low(normalize(x_pack) * (1.0 + scale_one) + shift_one)
    proj_three = jnp.einsum('sd,dcj->csj', h_one, wqkv, precision=highest)
    queries = low(low_back(proj_three[0] + bqv[0]))
    key_rows = low(low_back(proj_three[1]))
    value_rows = low(low_back(proj_three[2] + bqv[1]))
    q_heads = queries.reshape(TOK_DEV, HEADS, HEAD_DIM)
    k_heads = key_rows.reshape(TOK_DEV, HEADS, HEAD_DIM)
    v_heads = value_rows.reshape(TOK_DEV, HEADS, HEAD_DIM)
    scores = low_back(HEAD_DIM ** (-0.5) * jnp.einsum('qhe,khe->hqk', q_heads, k_heads, precision=highest))
    same_seg = seg_pack[:, None] == seg_pack[None, :]
    scores = jnp.where(same_seg[None], scores, -1e+30)
    expo = jnp.exp(scores - lax.optimization_barrier(jnp.max(scores, axis=-1, keepdims=True)))
    probs = expo / lax.optimization_barrier(jnp.sum(expo, axis=-1, keepdims=True))
    attended = jnp.einsum('hqk,khe->qhe', low(probs), v_heads, precision=highest).reshape(TOK_DEV, HEADS * HEAD_DIM)
    head_keep = jnp.repeat(jnp.dot(select, hmask_pack.astype(jnp.float32), precision=highest), HEAD_DIM, axis=1)
    attn_low = low(low_back(attended * head_keep))
    branch_a = low_back(jnp.dot(attn_low, wproj, precision=highest) + bproj)
    mid = x_pack + gate_one * branch_a
    h_two = low(normalize(mid) * (1.0 + scale_two) + shift_two)
    hidden = low_back(jnp.dot(h_two, wone, precision=highest) + bone)
    gelu_out = low(jax.nn.gelu(hidden, approximate=True))
    branch_m = low_back(jnp.dot(gelu_out, wtwo, precision=highest) + btwo)
    keep_col = keep_pack.astype(jnp.float32)[:, None]
    return mid + gate_two * keep_col * branch_m

def forward(seg_ids, time_steps, head_masks, skip_masks, x_all, ada_w, ada_b, wqkv, bqv, wproj, bproj, wone, bone, wtwo, btwo):
    time_act = low(jax.nn.silu(embed_steps(time_steps)))
    modulation = jnp.dot(time_act, ada_w, precision=highest) + ada_b
    mods = modulation.reshape(N_DP, SEG_DEV, 6 * D)
    x_packs = x_all.reshape(N_DP, TOK_DEV, D)
    hmasks = head_masks.reshape(N_DP, SEG_DEV, HEADS)
    weights = (wqkv, bqv, wproj, bproj, wone, bone, wtwo, btwo)
    layer_fn = jax.checkpoint(partial(pack_layer, weights))
    outs = lax.map(lambda packed: layer_fn(*packed), (x_packs, seg_ids, hmasks, skip_masks, mods))
    return outs.reshape(TOKENS, D)

def reference(tokens, seg_ids, time_steps, head_masks, skip_masks, ada_weight, ada_bias, qkv_weight, qv_bias, proj_weight, proj_bias, fc1_weight, fc1_bias, fc2_weight, fc2_bias, out_cotangent):
    floats = tuple((a.astype(jnp.float32) for a in (tokens, ada_weight, ada_bias, qkv_weight, qv_bias, proj_weight, proj_bias, fc1_weight, fc1_bias, fc2_weight, fc2_bias)))
    layer = partial(forward, seg_ids, time_steps, head_masks, skip_masks)
    result, pull = jax.vjp(layer, *floats)
    grads = pull(out_cotangent.astype(jnp.float32))
    return (result.astype(jnp.bfloat16), grads[0], grads[1], grads[2], grads[3], grads[4], grads[5], grads[6], grads[7], grads[8], grads[9], grads[10])
```

```python
import math

import jax
import jax.numpy as jnp
from jax import lax
from jax.sharding import PartitionSpec as P

HEAD_DIM = 72


highest = lax.Precision.HIGHEST


def embed_steps(steps, model_width):
    half_width = model_width // 2
    freqs = jnp.exp(-math.log(10000.0) * jnp.arange(half_width, dtype=jnp.float32) / half_width)
    angles = steps.astype(jnp.float32)[:, None] * freqs[None, :]
    return jnp.concatenate([jnp.cos(angles), jnp.sin(angles)], axis=1)


def normalize(value):
    center = value - jnp.mean(value, axis=-1, keepdims=True)
    return center * lax.rsqrt(jnp.mean(center * center, axis=-1, keepdims=True) + 1e-06)


def norm_back(value, grad):
    return jax.vjp(normalize, value)[1](grad)[0]


def gelu_tanh(value):
    return jax.nn.gelu(value, approximate=True)


def per_token(select, table):
    return jnp.dot(select, table, precision=highest)


def item_sums(select, values):
    return jnp.einsum("sg,sd->gd", select, values, precision=highest)


def attend_forward(queries, key_rows, value_rows, segment, heads_here, score_scale, block_rows):
    length = queries.shape[0]
    q_heads = queries.reshape(length, heads_here, -1)
    k_heads = key_rows.reshape(length, heads_here, -1)
    v_heads = value_rows.reshape(length, heads_here, -1)

    def one_block(start):
        q_block = lax.dynamic_slice_in_dim(q_heads, start, block_rows, 0)
        seg_query = lax.dynamic_slice_in_dim(segment, start, block_rows, 0)
        scores = (
            jnp.einsum("qhe,khe->hqk", q_block, k_heads, preferred_element_type=jnp.float32)
            * score_scale
        )
        scores = jnp.where((seg_query[:, None] == segment[None, :])[None], scores, -1e30)
        row_peak = jnp.max(scores, axis=-1, keepdims=True)
        row_exp = jnp.exp(scores - row_peak)
        row_total = jnp.sum(row_exp, axis=-1, keepdims=True)
        prob_low = (row_exp / row_total).astype(jnp.bfloat16)
        out_block = jnp.einsum(
            "hqk,khe->qhe", prob_low, v_heads, preferred_element_type=jnp.float32
        )
        return (out_block.reshape(block_rows, -1), (row_peak + jnp.log(row_total))[..., 0])

    starts = jnp.arange(length // block_rows, dtype=jnp.int32) * block_rows
    out_blocks, log_totals = lax.map(one_block, starts)
    return (out_blocks.reshape(length, -1), log_totals)


def attend_backward(
    queries,
    key_rows,
    value_rows,
    grad_attn,
    segment,
    log_totals,
    heads_here,
    score_scale,
    block_rows,
):
    length = queries.shape[0]
    q_heads = queries.reshape(length, heads_here, -1)
    k_heads = key_rows.reshape(length, heads_here, -1)
    v_heads = value_rows.reshape(length, heads_here, -1)
    g_heads = grad_attn.reshape(length, heads_here, -1)

    def one_block(carry, inputs):
        start, lse_block = inputs
        grad_keys_acc, grad_values_acc = carry
        q_block = lax.dynamic_slice_in_dim(q_heads, start, block_rows, 0)
        g_block = lax.dynamic_slice_in_dim(g_heads, start, block_rows, 0)
        seg_query = lax.dynamic_slice_in_dim(segment, start, block_rows, 0)
        scores = (
            jnp.einsum("qhe,khe->hqk", q_block, k_heads, preferred_element_type=jnp.float32)
            * score_scale
        )
        scores = jnp.where((seg_query[:, None] == segment[None, :])[None], scores, -1e30)
        probs = jnp.exp(scores - lse_block[..., None])
        grad_probs = jnp.einsum(
            "qhe,khe->hqk", g_block, v_heads, preferred_element_type=jnp.float32
        )
        row_delta = jnp.sum(grad_probs * probs, axis=-1, keepdims=True)
        grad_scores = (probs * (grad_probs - row_delta)).astype(jnp.bfloat16)
        grad_query = (
            jnp.einsum("hqk,khe->qhe", grad_scores, k_heads, preferred_element_type=jnp.float32)
            * score_scale
        )
        grad_keys_acc = grad_keys_acc + jnp.einsum(
            "hqk,qhe->khe", grad_scores, q_block, preferred_element_type=jnp.float32
        )
        grad_values_acc = grad_values_acc + jnp.einsum(
            "hqk,qhe->khe", probs.astype(jnp.bfloat16), g_block, preferred_element_type=jnp.float32
        )
        return (
            (grad_keys_acc, grad_values_acc),
            grad_query.astype(jnp.bfloat16).reshape(block_rows, -1),
        )

    starts = jnp.arange(length // block_rows, dtype=jnp.int32) * block_rows
    zeros_acc = jnp.zeros(k_heads.shape, jnp.float32)
    (grad_keys_acc, grad_values_acc), grad_query = lax.scan(
        one_block, (zeros_acc, zeros_acc), (starts, log_totals)
    )
    grad_keys = (grad_keys_acc * score_scale).astype(jnp.bfloat16).reshape(length, -1)
    grad_values = grad_values_acc.astype(jnp.bfloat16).reshape(length, -1)
    return (grad_query.reshape(length, -1), grad_keys, grad_values)


def local(
    tokens,
    seg_ids,
    time_steps,
    head_masks,
    skip_masks,
    ada_weight,
    ada_bias,
    qkv_weight,
    qv_bias,
    proj_weight,
    proj_bias,
    fc1_weight,
    fc1_bias,
    fc2_weight,
    fc2_bias,
    out_cotangent,
):
    length, model_width = tokens.shape
    groups = time_steps.shape[0]
    heads_here = qkv_weight.shape[2] // HEAD_DIM
    score_scale = HEAD_DIM ** (-0.5)
    block_rows = min(512, length)
    share_rows = length // lax.axis_size("head")
    row_start = lax.axis_index("head") * share_rows
    segment = seg_ids[0]
    keep_tok = skip_masks[0].astype(jnp.float32)[:, None]
    select = (segment[:, None] == jnp.arange(groups, dtype=jnp.int32)[None, :]).astype(jnp.float32)

    def own_rows(value):
        return lax.dynamic_slice_in_dim(value, row_start, share_rows, 0)

    time_act = jax.nn.silu(embed_steps(time_steps, model_width)).astype(jnp.bfloat16)
    mod_part = jnp.dot(time_act, ada_weight, preferred_element_type=jnp.float32) + ada_bias.astype(
        jnp.float32
    )
    modulation = lax.all_gather(mod_part, "head", axis=1, tiled=True)
    shift_one, scale_one = [
        per_token(select, modulation[:, k * model_width : (k + 1) * model_width]) for k in (0, 1)
    ]
    x_full = tokens.astype(jnp.float32)
    norm_one = normalize(x_full)
    h_one = (norm_one * (1.0 + scale_one) + shift_one).astype(jnp.bfloat16)
    proj_three = jnp.einsum("sd,dcj->csj", h_one, qkv_weight, preferred_element_type=jnp.float32)
    qv_float = qv_bias.astype(jnp.float32)
    queries = (proj_three[0] + qv_float[0]).astype(jnp.bfloat16)
    key_rows = proj_three[1].astype(jnp.bfloat16)
    value_rows = (proj_three[2] + qv_float[1]).astype(jnp.bfloat16)
    attended, log_totals = attend_forward(
        queries, key_rows, value_rows, segment, heads_here, score_scale, block_rows
    )
    head_keep = jnp.repeat(per_token(select, head_masks.astype(jnp.float32)), HEAD_DIM, axis=1)
    attn_low = (attended * head_keep).astype(jnp.bfloat16)
    proj_b = proj_bias.astype(jnp.float32)
    fc1_b = fc1_bias.astype(jnp.float32)
    fc2_b = fc2_bias.astype(jnp.float32)

    def scatter_sum(part):
        return lax.psum_scatter(
            part.astype(jnp.bfloat16), "head", scatter_dimension=0, tiled=True
        ).astype(jnp.float32)

    def share_rows_of(value):
        return lax.all_gather(value, "head", axis=0, tiled=True)

    attn_part = jnp.dot(attn_low, proj_weight, preferred_element_type=jnp.float32)
    branch_a = scatter_sum(attn_part) + proj_b
    x_own = own_rows(tokens).astype(jnp.float32)
    select_own = own_rows(select)
    keep_own = own_rows(keep_tok)
    cot_own = own_rows(out_cotangent).astype(jnp.float32)
    shift_one_o, scale_one_o, gate_one_o, shift_two_o, scale_two_o, gate_two_o = jnp.split(
        per_token(select_own, modulation), 6, axis=1
    )
    mid_rows = x_own + gate_one_o * branch_a
    norm_two = normalize(mid_rows)
    h_two = share_rows_of((norm_two * (1.0 + scale_two_o) + shift_two_o).astype(jnp.bfloat16))
    hidden = jnp.dot(h_two, fc1_weight, preferred_element_type=jnp.float32) + fc1_b
    gelu_out = gelu_tanh(hidden).astype(jnp.bfloat16)
    mlp_part = jnp.dot(gelu_out, fc2_weight, preferred_element_type=jnp.float32)
    gate_two = per_token(select, modulation[:, 5 * model_width :])
    grad_m = (out_cotangent.astype(jnp.float32) * gate_two * keep_tok).astype(jnp.bfloat16)
    grad_gelu = jnp.einsum("sd,fd->sf", grad_m, fc2_weight, preferred_element_type=jnp.float32)
    grad_hidden = jax.vjp(gelu_tanh, hidden)[1](grad_gelu)[0].astype(jnp.bfloat16)
    h_two_part = jnp.einsum(
        "sf,df->sd", grad_hidden, fc1_weight, preferred_element_type=jnp.float32
    )
    grad_h_two = scatter_sum(h_two_part)
    fc2_grad = jnp.einsum("sf,sd->fd", gelu_out, grad_m, preferred_element_type=jnp.float32)
    fc2_bias_grad = jnp.sum(grad_m.astype(jnp.float32), axis=0)
    fc1_grad = jnp.einsum("sd,sf->df", h_two, grad_hidden, preferred_element_type=jnp.float32)
    fc1_bias_grad = jnp.sum(grad_hidden.astype(jnp.float32), axis=0)
    branch_m = scatter_sum(mlp_part) + fc2_b
    layer_out = (mid_rows + gate_two_o * keep_own * branch_m).astype(jnp.bfloat16)
    gate_two_grad = item_sums(select_own, cot_own * keep_own * branch_m)
    grad_mid = cot_own + norm_back(mid_rows, grad_h_two * (1.0 + scale_two_o))
    shift_two_grad = item_sums(select_own, grad_h_two)
    scale_two_grad = item_sums(select_own, grad_h_two * norm_two)
    gate_one_grad = item_sums(select_own, grad_mid * branch_a)
    grad_a = share_rows_of((grad_mid * gate_one_o).astype(jnp.bfloat16))
    proj_bias_grad = jnp.sum(grad_a.astype(jnp.float32), axis=0)
    proj_grad = jnp.einsum("sj,sd->jd", attn_low, grad_a, preferred_element_type=jnp.float32)
    grad_attn_low = jnp.einsum(
        "sd,jd->sj", grad_a, proj_weight, preferred_element_type=jnp.float32
    ).astype(jnp.bfloat16)
    grad_attn = grad_attn_low * head_keep.astype(jnp.bfloat16)
    grad_queries, grad_keys, grad_values = attend_backward(
        queries,
        key_rows,
        value_rows,
        grad_attn,
        segment,
        log_totals,
        heads_here,
        score_scale,
        block_rows,
    )
    grad_three = jnp.stack([grad_queries, grad_keys, grad_values])
    qkv_grad = jnp.einsum("sd,csj->dcj", h_one, grad_three, preferred_element_type=jnp.float32)
    qv_bias_grad = jnp.stack(
        [
            jnp.sum(grad_queries.astype(jnp.float32), axis=0),
            jnp.sum(grad_values.astype(jnp.float32), axis=0),
        ]
    )
    h_one_part = jnp.einsum(
        "csj,dcj->sd", grad_three, qkv_weight, preferred_element_type=jnp.float32
    )
    grad_h_one = scatter_sum(h_one_part)
    input_grad = grad_mid + norm_back(x_own, grad_h_one * (1.0 + scale_one_o))
    shift_one_grad = item_sums(select_own, grad_h_one)
    scale_one_grad = item_sums(select_own, grad_h_one * normalize(x_own))
    mod_grad = jnp.concatenate(
        [
            shift_one_grad,
            scale_one_grad,
            gate_one_grad,
            shift_two_grad,
            scale_two_grad,
            gate_two_grad,
        ],
        axis=1,
    )
    mod_cols = lax.psum_scatter(mod_grad, "head", scatter_dimension=1, tiled=True)
    all_cols = lax.all_gather(mod_cols, "dp", axis=0, tiled=True)
    all_act = lax.all_gather(time_act, "dp", axis=0, tiled=True)
    ada_grad = jnp.einsum("gd,gc->dc", all_act.astype(jnp.float32), all_cols, precision=highest)
    ada_bias_grad = jnp.sum(all_cols, axis=0)
    summed = lax.psum(
        (
            qkv_grad.astype(jnp.bfloat16),
            proj_grad.astype(jnp.bfloat16),
            fc1_grad.astype(jnp.bfloat16),
            fc2_grad.astype(jnp.bfloat16),
        ),
        "dp",
    )
    qkv_grad, proj_grad, fc1_grad, fc2_grad = [g.astype(jnp.float32) for g in summed]
    qv_bias_grad, proj_bias_grad, fc1_bias_grad, fc2_bias_grad = lax.psum(
        (qv_bias_grad, proj_bias_grad, fc1_bias_grad, fc2_bias_grad), "dp"
    )
    return (
        layer_out,
        input_grad,
        ada_grad,
        ada_bias_grad,
        qkv_grad,
        qv_bias_grad,
        proj_grad,
        proj_bias_grad,
        fc1_grad,
        fc1_bias_grad,
        fc2_grad,
        fc2_bias_grad,
    )


def solution(mesh):
    placed = (
        P("dp", None),
        P("dp", None),
        P("dp"),
        P("dp", "head"),
        P("dp", None),
        P(None, "head"),
        P("head"),
        P(None, None, "head"),
        P(None, "head"),
        P("head", None),
        P(),
        P(None, "head"),
        P("head"),
        P("head", None),
        P(),
        P("dp", None),
    )
    return jax.shard_map(
        local,
        mesh=mesh,
        in_specs=placed,
        out_specs=(
            P(("dp", "head"), None),
            P(("dp", "head"), None),
            P(None, "head"),
            P("head"),
            P(None, None, "head"),
            P(None, "head"),
            P("head", None),
            P(),
            P(None, "head"),
            P("head"),
            P("head", None),
            P(),
        ),
        check_vma=False,
    )
```
